32 devices in a mesh: expert: 4 (over y, core), fsdp: 8 (over z, x).
Axes of the slice: x: 2, y: 2, z: 4, core: 2. Of those that a mesh axis runs over, the one named last changes fastest.
Arguments:
- layer_input: bfloat16 [8192, 2048], P(('expert', 'fsdp')), may hold values from -6 to 6
- expert_ids: int32 [8192, 8], P(('expert', 'fsdp')), may hold values from 0 to 15, as said below
- slot_ids: int32 [8192, 8], P(('expert', 'fsdp')), may hold values from 0 to 255, as said below
- attn_gain: float32 [2048], replicated, may hold values from 0.25 to 1.75
- qkv_weight: bfloat16 [2048, 6144], P('fsdp'), may hold values from -0.125 to 0.125
- query_gain: float32 [128], replicated, may hold values from 0.25 to 1.75
- key_gain: float32 [128], replicated, may hold values from 0.25 to 1.75
- out_weight: bfloat16 [2048, 2048], P('fsdp'), may hold values from -1 to 1
- ffn_gain: float32 [2048], replicated, may hold values from 0.25 to 1.75
- router_weight: bfloat16 [2048, 16], P('fsdp'), may hold values from -0.0625 to 0.0625
- gate_up_weight: bfloat16 [16, 2048, 2048], P('expert', 'fsdp'), may hold values from -0.125 to 0.125
- down_weight: bfloat16 [16, 1024, 2048], P('expert', 'fsdp'), may hold values from -0.75 to 0.75
- cotangent: bfloat16 [8192, 2048], P(('expert', 'fsdp')), may hold values from -6 to 6
Outputs:
- mixed_out: bfloat16 [8192, 2048], P(('expert', 'fsdp'))
- input_grad: float32 [8192, 2048], P(('expert', 'fsdp'))
- attn_gain_grad: float32 [2048], replicated
- qkv_weight_grad: float32 [2048, 6144], P('fsdp')
- query_gain_grad: float32 [128], replicated
- key_gain_grad: float32 [128], replicated
- out_weight_grad: float32 [2048, 2048], P('fsdp')
- ffn_gain_grad: float32 [2048], replicated
- router_weight_grad: float32 [2048, 16], P('fsdp')
- gate_up_grad: float32 [16, 2048, 2048], P('expert', 'fsdp')
- down_grad: float32 [16, 1024, 2048], P('expert', 'fsdp')
The draws below stay inside these ranges and needn't reach their ends.
Inputs may be any that keep to these rules, and one draw needn't show every extreme that they name: `expert_ids`: each row names 8 different experts. Among the 256 rows of one device no expert is named more than 256 times; in every device's rows one expert is named exactly 256 times. `slot_ids`: among the rows of one device, the routes to one expert have different slots.
All inputs are finite; a program needn't handle non-finite values.
Results may differ from the reference program's by a relative error of at most 0.022.
Values may be sent and summed in bfloat16 or wider, within the bound.
No kernel may reach another device: no remote copies, remote signals or barrier semaphores. Data moves between devices by JAX's collectives and lax.ppermute only.
A program may use at most 384 MiB of HBM per device.

```python
import jax
import jax.numpy as jnp
from jax import lax

D = 2048
H = 16
HD = 128
FF = 1024
TOPK = 8
TOK_DEV = 256
EXPERTS = 16
CAP = 256
TOKENS = 8192


def layout(key):
    blocks = TOKENS // TOK_DEV
    mean_load = TOK_DEV * TOPK // EXPERTS
    stride = 2 * mean_load // EXPERTS
    half_count = EXPERTS // 2
    rank_ids = jnp.arange(EXPERTS, dtype=jnp.int32)
    pair_index = jnp.minimum(rank_ids, EXPERTS - 1 - rank_ids)
    signed = jnp.where(rank_ids < half_count, 1, -1).astype(jnp.int32)
    base_load = mean_load + signed * stride * (half_count - pair_index)
    streams = jax.random.split(jax.random.fold_in(key, 7), 5)
    jitter = jax.random.randint(streams[0], (blocks, half_count), 0, max(stride, 1)).astype(jnp.int32)
    jitter = jitter.at[:, 0].set(0)
    load_counts = base_load[None, :] - signed[None, :] * jitter[:, pair_index]
    run_ends = jnp.cumsum(load_counts, 1)
    starts = run_ends - load_counts
    position = jnp.arange(TOK_DEV * TOPK, dtype=jnp.int32)
    run_index = jnp.sum((run_ends[:, None, :] <= position[None, :, None]).astype(jnp.int32), 2)
    offset = position[None, :] - jnp.take_along_axis(starts, run_index, 1)
    heavy_expert = jax.random.randint(streams[1], (), 0, EXPERTS).astype(jnp.int32)

    def relabel(stream):
        label_order = jax.random.permutation(stream, EXPERTS).astype(jnp.int32)
        heavy_spot = jnp.argmax(label_order == heavy_expert)
        return label_order.at[heavy_spot].set(label_order[0]).at[0].set(heavy_expert)
    labels = jax.vmap(relabel)(jax.random.split(streams[2], blocks))
    chosen = jnp.take_along_axis(labels, run_index, 1)
    chosen = chosen.reshape(blocks, TOPK, TOK_DEV).transpose(0, 2, 1)
    offset = offset.reshape(blocks, TOPK, TOK_DEV).transpose(0, 2, 1)
    scores = jax.random.randint(streams[3], (blocks, TOK_DEV, TOPK), 0, 4096).astype(jnp.int32) * TOPK + jnp.arange(TOPK, dtype=jnp.int32)
    column = jnp.argsort(scores, -1)
    chosen = jnp.take_along_axis(chosen, column, 2)
    offset = jnp.take_along_axis(offset, column, 2)

    def shuffle(stream):
        return jax.random.permutation(stream, TOK_DEV).astype(jnp.int32)
    row_order = jax.vmap(shuffle)(jax.random.split(streams[4], blocks))
    chosen = jnp.take_along_axis(chosen, row_order[:, :, None], 1)
    offset = jnp.take_along_axis(offset, row_order[:, :, None], 1)
    return (chosen.reshape(TOKENS, TOPK).astype(jnp.int32), offset.reshape(TOKENS, TOPK).astype(jnp.int32))


def draw_expert_ids(key, part):
    return layout(key)[0]


def draw_slot_ids(key, part):
    return layout(key)[1]


def spiked(entries, stream_key, source, target, shards_of, factor):
    owner, partner = [(jnp.arange(entries.shape[dim]) // (entries.shape[dim] // shards_of)).reshape([-1 if axis == dim else 1 for axis in range(entries.ndim)]) for dim in (source, target)]
    chosen = jax.random.permutation(stream_key, shards_of)[partner]
    strong = (owner == chosen) | (owner == (partner + shards_of // 2) % shards_of)
    return jnp.where(strong, factor * entries, entries)


def block_levels(rng, shape, shards, smallest, top_value):
    level, own = 1.0, jax.random.fold_in(rng, 6)
    for dim, parts in shards:
        heights = jnp.exp(jax.random.uniform(jax.random.fold_in(own, dim), (parts,), jnp.float32, smallest / len(shards), top_value / len(shards)))
        level = level * jnp.repeat(heights, shape[dim] // parts).reshape([-1 if axis == dim else 1 for axis in range(len(shape))])
    return level


def normal_values(own_key, shape, spread, reach, cuts=(), kind=jnp.bfloat16):
    result = jax.random.normal(own_key, shape, jnp.float32) * spread
    if len(cuts) > 0:
        result = block_levels(own_key, shape, cuts, -0.22, 0.18) * result
    return jnp.clip(result, min=-reach, max=reach).astype(kind)


def noise_with(stream_key, dims, scale, most, shards, heavy, kind=jnp.bfloat16):
    result = scale * jax.random.normal(stream_key, dims, jnp.float32)
    if shards:
        result = result * block_levels(stream_key, dims, shards, -0.22, 0.18)
    return jnp.clip(spiked(result, jax.random.fold_in(stream_key, 3), *heavy), -most, most).astype(kind)


def setup_inputs(seed: int = 0) -> dict:
    key_list = jax.random.split(jax.random.key(seed), 14)
    return {
        "layer_input": noise_with(key_list[0], (TOKENS, D), 1.0, 6.0, ((0, 32),), (0, 1, 32, 2.75)),
        "expert_ids": draw_expert_ids(jax.random.fold_in(key_list[13], 71), 0),
        "slot_ids": draw_slot_ids(jax.random.fold_in(key_list[13], 71), 0),
        "attn_gain": jnp.clip(1.0 + 0.15 * jax.random.normal(key_list[3], (D,), jnp.float32), 0.25, 1.75),
        "qkv_weight": normal_values(key_list[4], (D, 3 * D), D ** -0.5, 0.125, ((0, 8),)),
        "query_gain": jnp.clip(1.0 + 0.15 * jax.random.normal(key_list[5], (HD,), jnp.float32), 0.25, 1.75),
        "key_gain": jnp.clip(1.0 + 0.15 * jax.random.normal(key_list[6], (HD,), jnp.float32), 0.25, 1.75),
        "out_weight": normal_values(key_list[7], (D, D), (D * 4 // TOK_DEV) ** -0.5, 1.0, ((0, 8),)),
        "ffn_gain": jnp.clip(1.0 + 0.15 * jax.random.normal(key_list[8], (D,), jnp.float32), 0.25, 1.75),
        "router_weight": normal_values(key_list[9], (D, EXPERTS), (4 * D) ** -0.5, 0.0625, ((0, 8),)),
        "gate_up_weight": normal_values(key_list[10], (EXPERTS, D, 2 * FF), D ** -0.5, 0.125, ((0, 4), (1, 8))),
        "down_weight": normal_values(key_list[11], (EXPERTS, FF, D), (FF // 16) ** -0.5, 0.75, ((0, 4), (1, 8))),
        "cotangent": normal_values(key_list[12], (TOKENS, D), 1.0, 6.0, ((0, 32),)),
    }


EPSILON = 1e-06
ROPE_BASE = 50000.0
PRECISE = lax.Precision.HIGHEST

@jax.custom_vjp
def low(v):
    return lax.optimization_barrier(v.astype(jnp.bfloat16)).astype(jnp.float32)

@jax.custom_vjp
def low_back(v):
    return v

def low_keep(v):
    return (low(v), None)

def low_pass(kept, grad):
    return (grad,)

def back_keep(v):
    return (v, None)

def back_low(kept, grad):
    return (low(grad),)
low.defvjp(low_keep, low_pass)
low_back.defvjp(back_keep, back_low)

def matmul(left, right):
    return jnp.dot(left, right, precision=PRECISE)

def rms_unit(values):
    return values * lax.rsqrt(lax.optimization_barrier(jnp.mean(values * values, -1, keepdims=True)) + EPSILON)

def tables(length, head_size):
    half_size = head_size // 2
    frequency = ROPE_BASE ** (-(jnp.arange(half_size, dtype=jnp.float32) * 2.0 / head_size))
    angles = jnp.arange(length, dtype=jnp.float32)[:, None] * frequency[None, :]
    angles = jnp.concatenate([angles, angles], 1)
    return (jnp.cos(angles)[:, None, :], jnp.sin(angles)[:, None, :])

def rotate(values, cos_table, sine_table):
    half_size = values.shape[-1] // 2
    turned = jnp.concatenate([-values[..., half_size:], values[..., :half_size]], -1)
    return values * cos_table + turned * sine_table

def group_forward(source, expert_ids, slot_ids, params):
    attn_gain, qkv_weight, query_gain, key_gain, out_weight, ffn_gain, router_weight, gate_up_weight, down_weight = params
    group_size = source.shape[0]
    row_count = group_size * TOK_DEV
    score_scale = HD ** (-0.5)
    flat_rows = source.reshape(row_count, D)
    normed = low(rms_unit(flat_rows) * attn_gain)
    projected = low_back(matmul(normed, qkv_weight))
    queries = projected[:, :D].reshape(group_size, TOK_DEV, H, HD)
    keys_raw = projected[:, D:2 * D].reshape(group_size, TOK_DEV, H, HD)
    values_raw = projected[:, 2 * D:].reshape(group_size, TOK_DEV, H, HD)
    cos_table, sine_table = tables(TOK_DEV, HD)
    query_rot = low(rotate(rms_unit(queries) * query_gain, cos_table, sine_table))
    key_rot = low(rotate(rms_unit(keys_raw) * key_gain, cos_table, sine_table))
    value_low = low(values_raw)
    scores = low_back(jnp.einsum('gqhd,gkhd->ghqk', query_rot, key_rot, precision=PRECISE) * score_scale)
    prob_low = low(jax.nn.softmax(scores, -1))
    mixed_heads = jnp.einsum('ghqk,gkhd->gqhd', prob_low, value_low, precision=PRECISE).reshape(row_count, D)
    mixed_heads = low(low_back(mixed_heads))
    residual = flat_rows + low_back(matmul(mixed_heads, out_weight))
    normed_two = low(rms_unit(residual) * ffn_gain)
    logits = low_back(matmul(normed_two, router_weight))
    routes = expert_ids.reshape(row_count, TOPK)
    gate_probs = jax.nn.softmax(jnp.take_along_axis(logits, routes, 1), -1)
    block_ids = (jnp.arange(row_count, dtype=jnp.int32) // TOK_DEV)[:, None]
    slot_index = (routes * (group_size * CAP) + block_ids * CAP + slot_ids.reshape(row_count, TOPK)).reshape(-1)
    copies = jnp.broadcast_to(normed_two[:, None, :], (row_count, TOPK, D)).reshape(row_count * TOPK, D)
    buffer = jnp.zeros((EXPERTS * group_size * CAP, D), normed_two.dtype).at[slot_index].set(copies)
    arrived = low_back(buffer).reshape(EXPERTS, group_size * CAP, D)
    gate_up_val = low_back(jnp.einsum('erd,edf->erf', arrived, gate_up_weight, precision=PRECISE))
    activated = low(jax.nn.silu(gate_up_val[..., :FF]) * gate_up_val[..., FF:])
    expert_out = jnp.einsum('erf,efd->erd', activated, down_weight, precision=PRECISE)
    expert_out = low_back(low(expert_out)).reshape(EXPERTS * group_size * CAP, D)
    picked = expert_out[slot_index].reshape(row_count, TOPK, D)
    moe_sum = lax.optimization_barrier(jnp.sum(gate_probs[:, :, None] * picked, 1))
    return (residual + moe_sum).reshape(group_size, TOK_DEV, D)

def reference(layer_input, expert_ids, slot_ids, attn_gain, qkv_weight, query_gain, key_gain, out_weight, ffn_gain, router_weight, gate_up_weight, down_weight, cotangent):
    blocks = TOKENS // TOK_DEV
    group_size = 1
    for option in range(1, blocks + 1):
        if blocks % option == 0 and option * TOK_DEV <= 1024:
            group_size = option
    groups = blocks // group_size
    params = tuple((tensor.astype(jnp.float32) for tensor in (attn_gain, qkv_weight, query_gain, key_gain, out_weight, ffn_gain, router_weight, gate_up_weight, down_weight)))
    source = layer_input.astype(jnp.float32).reshape(groups, group_size, TOK_DEV, D)
    routes = expert_ids.reshape(groups, group_size, TOK_DEV, TOPK)
    places = slot_ids.reshape(groups, group_size, TOK_DEV, TOPK)

    def forward_all(source_all, param_all):

        def forward_one(bundle):
            return group_forward(bundle[0], bundle[1], bundle[2], param_all)
        return lax.map(jax.checkpoint(forward_one), (source_all, routes, places))
    output, pullback = jax.vjp(forward_all, source, params)
    input_grad, gradients = pullback(cotangent.astype(jnp.float32).reshape(output.shape))
    return (output.reshape(TOKENS, D).astype(jnp.bfloat16), input_grad.reshape(TOKENS, D), gradients[0], gradients[1], gradients[2], gradients[3], gradients[4], gradients[5], gradients[6], gradients[7], gradients[8])
```

```python
import math

import jax
import jax.numpy as jnp
from jax import lax
from jax.sharding import Mesh, PartitionSpec as P

EPSILON = 1e-06
ROPE_BASE = 50000.0
F32 = jnp.float32
BF16 = jnp.bfloat16
LANES = 128


def dot(left, right, out=F32):
    return jnp.dot(left, right, preferred_element_type=F32).astype(out)


def dot_nt(left, right, out=F32):
    return lax.dot_general(
        left, right, (((1,), (1,)), ((), ())), preferred_element_type=F32
    ).astype(out)


def dot_tn(left, right, out=F32):
    return lax.dot_general(
        left, right, (((0,), (0,)), ((), ())), preferred_element_type=F32
    ).astype(out)


def normalize(values):
    factor = lax.rsqrt(jnp.mean(values * values, -1, keepdims=True) + EPSILON)
    return (values * factor, factor)


def norm_back(grad_unit, unit_val, factor):
    return factor * (grad_unit - unit_val * jnp.mean(grad_unit * unit_val, -1, keepdims=True))


def tables(length, head_size):
    half_size = head_size // 2
    frequency = ROPE_BASE ** (-(jnp.arange(half_size, dtype=F32) * 2.0 / head_size))
    angles = jnp.arange(length, dtype=F32)[:, None] * frequency[None, :]
    angles = jnp.concatenate([angles, angles], 1)
    return (jnp.cos(angles)[:, None, :], jnp.sin(angles)[:, None, :])


def rotate(values, cos_table, sine_table):
    half_size = values.shape[-1] // 2
    turned = jnp.concatenate([-values[..., half_size:], values[..., :half_size]], -1)
    return values * cos_table + turned * sine_table


def rotate_back(gradient, cos_table, sine_table):
    half_size = gradient.shape[-1] // 2
    turned_grad = gradient * sine_table
    return gradient * cos_table + jnp.concatenate(
        [turned_grad[..., half_size:], -turned_grad[..., :half_size]], -1
    )


def take(array, index):
    return lax.dynamic_index_in_dim(array, index, 0, keepdims=False)


def put(array, part, index):
    return lax.dynamic_update_index_in_dim(array, part, index, 0)


def shift(value, axis, size, step):
    return lax.ppermute(value, axis, [(i, (i + step) % size) for i in range(size)])


def exchange(blocks, axis, size):
    me = lax.axis_index(axis)
    result = put(jnp.zeros_like(blocks), take(blocks, me), me)
    for step in range(1, size):
        moved = shift(take(blocks, (me + step) % size), axis, size, step)
        result = put(result, moved, (me - step) % size)
    return result


def gather_square(own):
    my_y, my_b = lax.axis_index("y"), lax.axis_index("b")
    half = own.shape[0] // 2
    over_b = shift(own, "b", 2, 1)
    over_y = shift(own, "y", 2, 1)
    far = jnp.concatenate([shift(over_y[:half], "b", 2, 1), shift(over_b[half:], "y", 2, 1)], 0)
    same_y = jnp.where(my_b == 0, jnp.stack([own, over_b]), jnp.stack([over_b, own]))
    other_y = jnp.where(my_b == 0, jnp.stack([over_y, far]), jnp.stack([far, over_y]))
    return same_y, other_y


def add(left, right):
    return (left.astype(F32) + right.astype(F32)).astype(BF16)


def scatter_square(same_y, other_y):
    my_b = lax.axis_index("b")
    half = same_y.shape[1] // 2
    far = take(other_y, 1 - my_b)
    for_y = take(other_y, my_b)
    for_b = take(same_y, 1 - my_b)
    got_b = shift(far[:half], "b", 2, 1)
    got_y = shift(far[half:], "y", 2, 1)
    for_y = jnp.concatenate([add(for_y[:half], got_b), for_y[half:]], 0)
    for_b = jnp.concatenate([for_b[:half], add(for_b[half:], got_y)], 0)
    got_y = shift(for_y, "y", 2, 1)
    got_b = shift(for_b, "b", 2, 1)
    return (take(same_y, my_b).astype(F32) + got_y.astype(F32) + got_b.astype(F32)).astype(BF16)


def build(y_size, c_size, a_size, b_size):
    square = y_size == 2 and b_size == 2
    everywhere = ("a", "b", "y", "c")

    def reduce_rows(left, right):
        tokens, width = left.shape
        columns = right.shape[1]
        left = left.reshape(tokens, a_size, b_size, y_size, c_size, -1)
        piece = left.shape[-1]
        left = left.transpose(4, 0, 3, 2, 1, 5).reshape(c_size, tokens, width // c_size)
        my_c, my_y = lax.axis_index("c"), lax.axis_index("y")
        other = dot_tn(take(left, 1 - my_c), right, BF16)
        got = shift(other, "c", c_size, 1)
        mine = dot_tn(take(left, my_c), right)
        mine = (mine + got.astype(F32)).astype(BF16)
        mine = mine.reshape(y_size, b_size, a_size * piece, columns)
        if square:
            mine = scatter_square(take(mine, my_y), take(mine, 1 - my_y))
        else:
            mine = mine.reshape(y_size * b_size * a_size * piece, columns)
            mine = lax.psum_scatter(mine, ("y", "b"), scatter_dimension=0, tiled=True)
        mine = lax.psum_scatter(mine, "a", scatter_dimension=0, tiled=True)
        return lax.all_gather(mine, ("y", "c"), axis=0, tiled=True)

    def local(
        layer_input,
        expert_ids,
        slot_ids,
        attn_gain,
        qkv_weight,
        query_gain,
        key_gain,
        out_weight,
        ffn_gain,
        router_weight,
        gate_up_weight,
        down_weight,
        cotangent,
    ):
        tokens, model_width = layer_input.shape
        head_size = query_gain.shape[0]
        head_count = model_width // head_size
        experts = router_weight.shape[1]
        held, d_block, both = gate_up_weight.shape
        hidden = both // 2
        f_block = down_weight.shape[1]
        share = held // a_size
        score_scale = head_size ** (-0.5)
        my_y, my_c = lax.axis_index("y"), lax.axis_index("c")
        my_a, my_b = lax.axis_index("a"), lax.axis_index("b")

        part = qkv_weight.shape[0] // (y_size * c_size)
        spot = (my_y * c_size + my_c) * part
        qkv_full = lax.all_gather(
            lax.dynamic_slice_in_dim(qkv_weight, spot, part, 0), everywhere, axis=0, tiled=True
        )
        out_full = lax.all_gather(
            lax.dynamic_slice_in_dim(out_weight, spot, part, 0), everywhere, axis=0, tiled=True
        )
        router_full = lax.all_gather(router_weight, ("a", "b"), axis=0, tiled=True)

        def reorder(values):
            shape = values.shape[:-1]
            values = values.reshape(*shape, 2, a_size, b_size, f_block)
            return values.swapaxes(-3, -2).reshape(*shape, both)

        gate_up_sent = exchange(
            reorder(gate_up_weight).reshape(a_size, share, d_block, both), "a", a_size
        ).transpose(1, 0, 2, 3)
        down_sent = exchange(
            down_weight.reshape(a_size, share, f_block, model_width), "a", a_size
        ).transpose(1, 0, 2, 3)
        gate_up_sent = gate_up_sent.reshape(share * a_size * d_block, both)
        down_sent = down_sent.reshape(share * a_size * f_block, model_width)
        if square:
            gate_up_list = [
                half.reshape(b_size, share, a_size * d_block, both)
                for half in gather_square(gate_up_sent)
            ]
            down_list = [
                half.reshape(b_size, share, a_size * f_block, model_width)
                for half in gather_square(down_sent)
            ]
            owners = [my_y, 1 - my_y]
        else:
            gate_up_all = lax.all_gather(gate_up_sent, ("y", "b"), axis=0, tiled=True)
            down_all = lax.all_gather(down_sent, ("y", "b"), axis=0, tiled=True)
            gate_up_all = gate_up_all.reshape(y_size, b_size, share, a_size * d_block, both)
            down_all = down_all.reshape(y_size, b_size, share, a_size * f_block, model_width)
            gate_up_list = [gate_up_all[i] for i in range(y_size)]
            down_list = [down_all[i] for i in range(y_size)]
            owners = list(range(y_size))
        weights = []
        for owner, gate_up_part, down_part in zip(owners, gate_up_list, down_list):
            for s in range(share):
                number = ((owner * c_size + my_c) * a_size + my_a) * share + s
                weights.append(
                    (
                        number,
                        gate_up_part[:, s].reshape(model_width, both),
                        down_part[:, s].reshape(hidden, model_width),
                    )
                )

        upstream_all = lax.all_gather(cotangent, ("a", "c"), axis=0, tiled=True)

        source = layer_input.astype(F32)
        unit_one, factor_one = normalize(source)
        normed = (unit_one * attn_gain).astype(BF16)
        projected = dot(normed, qkv_full)
        queries = projected[:, :model_width].reshape(tokens, head_count, head_size)
        keys_raw = projected[:, model_width : 2 * model_width].reshape(
            tokens, head_count, head_size
        )
        values_raw = projected[:, 2 * model_width :].reshape(tokens, head_count, head_size)
        unit_query, factor_query = normalize(queries)
        unit_key, factor_key = normalize(keys_raw)
        cos_table, sine_table = tables(tokens, head_size)
        query_rot = rotate(unit_query * query_gain, cos_table, sine_table).astype(BF16)
        key_rot = rotate(unit_key * key_gain, cos_table, sine_table).astype(BF16)
        value_low = values_raw.astype(BF16)
        scores = (
            jnp.einsum("qhd,khd->hqk", query_rot, key_rot, preferred_element_type=F32)
            * score_scale
        )
        top_score = jnp.max(scores, -1, keepdims=True)
        weights_raw = jnp.exp(scores - top_score)
        totals = jnp.sum(weights_raw, -1, keepdims=True)
        prob_full = weights_raw / totals
        prob_low = prob_full.astype(BF16)
        mixed_heads = jnp.einsum("hqk,khd->qhd", prob_low, value_low, preferred_element_type=F32)
        mixed_low = mixed_heads.reshape(tokens, model_width).astype(BF16)
        residual = source + dot(mixed_low, out_full)
        unit_two, factor_two = normalize(residual)
        normed_two = (unit_two * ffn_gain).astype(BF16)
        logits = dot(normed_two, router_full)
        onehot = (
            expert_ids[:, :, None] == jnp.arange(experts, dtype=jnp.int32)[None, None, :]
        ).astype(F32)
        chosen = jnp.sum(onehot * logits[:, None, :], -1)
        gate_probs = jax.nn.softmax(chosen, -1)
        gate_dense = jnp.sum(onehot * gate_probs[:, :, None], 1)

        def swap_blocks(values, first, second):
            rows = values.shape[0]
            values = values.reshape(rows, first, second, d_block)
            return values.transpose(0, 2, 1, 3).reshape(rows, model_width)

        def split(values):
            high = values.astype(BF16)
            low = (values - high.astype(F32)).astype(BF16)
            pad = jnp.zeros((values.shape[0], LANES - 2 * experts), BF16)
            return jnp.concatenate([high, low, pad], 1)

        def join(values):
            return values[:, :experts].astype(F32) + values[:, experts : 2 * experts].astype(F32)

        rows_sent = jnp.concatenate(
            [swap_blocks(normed_two, a_size, b_size), split(gate_dense)], 1
        )
        rows_all = lax.all_gather(rows_sent, ("a", "c"), axis=0, tiled=True)
        rows_in = rows_all[:, :model_width]
        gates_all = join(rows_all[:, model_width:])
        numbers = jnp.arange(experts, dtype=jnp.int32)[None, :]
        moe_part = 0.0
        row_part = 0.0
        gate_grad_part = jnp.zeros((rows_all.shape[0], experts), F32)
        grads = []
        for number, gate_up_full, down_full in weights:
            mask = (numbers == number).astype(F32)
            gate_here = jnp.sum(gates_all * mask, 1, keepdims=True)
            gate_up_val = dot(rows_in, gate_up_full)
            gate_part = gate_up_val[:, :hidden]
            up_part = gate_up_val[:, hidden:]
            sigmoid_gate = jax.nn.sigmoid(gate_part)
            activated = gate_part * sigmoid_gate * up_part
            act_grad = dot_nt(upstream_all, down_full)
            gate_grad_part = gate_grad_part + mask * jnp.sum(
                activated * act_grad, -1, keepdims=True
            )
            act_gated = (gate_here * activated).astype(BF16)
            act_grad = gate_here * act_grad
            gate_side = act_grad * up_part * sigmoid_gate * (1.0 + gate_part * (1.0 - sigmoid_gate))
            up_side = act_grad * gate_part * sigmoid_gate
            both_grad = jnp.concatenate([gate_side, up_side], -1).astype(BF16)
            row_part = row_part + dot_nt(both_grad, gate_up_full)
            moe_part = moe_part + dot(act_gated, down_full)
            grads.append(
                (dot_tn(rows_in, both_grad, BF16), dot_tn(act_gated, upstream_all, BF16))
            )
        back_sent = jnp.concatenate([row_part.astype(BF16), split(gate_grad_part)], 1)
        back = lax.psum_scatter(back_sent, ("a", "c"), scatter_dimension=0, tiled=True)
        moe_sum = lax.psum_scatter(
            moe_part.astype(BF16), ("a", "c"), scatter_dimension=0, tiled=True
        )
        mixed_out = (residual + moe_sum.astype(F32)).astype(BF16)

        def home(parts, block):
            columns = parts[0].shape[1]
            parts = [
                jnp.stack(parts[i * share : (i + 1) * share]).reshape(
                    share, b_size, a_size * block, columns
                )
                for i in range(y_size)
            ]
            parts = [p.swapaxes(0, 1).reshape(b_size, share * a_size * block, columns) for p in parts]
            if square:
                summed = scatter_square(parts[0], parts[1])
            else:
                summed = lax.psum_scatter(
                    jnp.stack(parts).reshape(-1, columns),
                    ("y", "b"),
                    scatter_dimension=0,
                    tiled=True,
                )
            summed = summed.reshape(share, a_size, block, columns).swapaxes(0, 1)
            return exchange(summed, "a", a_size).reshape(held, block, columns)

        gate_up_grad = home([g[0] for g in grads], d_block)
        down_grad = home([g[1] for g in grads], f_block).astype(F32)
        gate_up_grad = gate_up_grad.reshape(held, d_block, 2, b_size, a_size, f_block)
        gate_up_grad = gate_up_grad.swapaxes(3, 4).reshape(held, d_block, both).astype(F32)

        upstream = cotangent.astype(F32)
        gate_grad = join(back[:, model_width:])
        mean_grad = jnp.sum(gate_dense * gate_grad, -1, keepdims=True)
        logit_grad = (gate_dense * (gate_grad - mean_grad)).astype(BF16)
        normed_two_grad = swap_blocks(back[:, :model_width], b_size, a_size).astype(
            F32
        ) + dot_nt(logit_grad, router_full)
        ffn_gain_part = jnp.sum(normed_two_grad * unit_two, 0)
        residual_grad = upstream + norm_back(normed_two_grad * ffn_gain, unit_two, factor_two)
        attn_grad_low = residual_grad.astype(BF16)
        router_grad_full = dot_tn(normed_two, logit_grad, BF16)
        router_shard = lax.psum_scatter(
            router_grad_full, ("a", "b"), scatter_dimension=0, tiled=True
        )
        router_weight_grad = lax.psum(router_shard, ("y", "c")).astype(F32)
        out_weight_grad = reduce_rows(mixed_low, attn_grad_low).astype(F32)
        mixed_grad = dot_nt(attn_grad_low, out_full, BF16)
        mixed_grad = mixed_grad.reshape(tokens, head_count, head_size)
        value_grad = jnp.einsum("hqk,qhd->khd", prob_low, mixed_grad, preferred_element_type=F32)
        prob_grad = jnp.einsum("qhd,khd->hqk", mixed_grad, value_low, preferred_element_type=F32)
        score_grad = (
            prob_full * (prob_grad - jnp.sum(prob_full * prob_grad, -1, keepdims=True))
        ).astype(BF16)
        query_grad = (
            jnp.einsum("hqk,khd->qhd", score_grad, key_rot, preferred_element_type=F32)
            * score_scale
        )
        key_grad = (
            jnp.einsum("hqk,qhd->khd", score_grad, query_rot, preferred_element_type=F32)
            * score_scale
        )
        query_grad = rotate_back(query_grad, cos_table, sine_table)
        key_grad = rotate_back(key_grad, cos_table, sine_table)
        query_gain_part = jnp.sum(query_grad * unit_query, (0, 1))
        key_gain_part = jnp.sum(key_grad * unit_key, (0, 1))
        query_pre = norm_back(query_grad * query_gain, unit_query, factor_query)
        key_pre = norm_back(key_grad * key_gain, unit_key, factor_key)
        qkv_grad_low = jnp.concatenate(
            [
                query_pre.reshape(tokens, model_width),
                key_pre.reshape(tokens, model_width),
                value_grad.reshape(tokens, model_width),
            ],
            1,
        ).astype(BF16)
        qkv_weight_grad = reduce_rows(normed, qkv_grad_low).astype(F32)
        normed_grad = dot_nt(qkv_grad_low, qkv_full)
        attn_gain_part = jnp.sum(normed_grad * unit_one, 0)
        input_grad = residual_grad + norm_back(normed_grad * attn_gain, unit_one, factor_one)
        gains = jnp.concatenate([attn_gain_part, ffn_gain_part, query_gain_part, key_gain_part])
        gains = jnp.sum(lax.all_gather(gains[None], everywhere, axis=0, tiled=True), 0)
        attn_gain_grad = gains[:model_width]
        ffn_gain_grad = gains[model_width : 2 * model_width]
        query_gain_grad = gains[2 * model_width : 2 * model_width + head_size]
        key_gain_grad = gains[2 * model_width + head_size :]
        return (
            mixed_out,
            input_grad,
            attn_gain_grad,
            qkv_weight_grad,
            query_gain_grad,
            key_gain_grad,
            out_weight_grad,
            ffn_gain_grad,
            router_weight_grad,
            gate_up_grad,
            down_grad,
        )

    return local


def solution(mesh):
    c_size, a_size = 2, 4
    y_size = mesh.shape["expert"] // c_size
    b_size = mesh.shape["fsdp"] // a_size
    fine = Mesh(mesh.devices.reshape(y_size, c_size, a_size, b_size), ("y", "c", "a", "b"))
    rows, model, held = P(("y", "c", "a", "b"), None), P(("a", "b"), None), P(("y", "c"), ("a", "b"), None)
    return jax.shard_map(
        build(y_size, c_size, a_size, b_size),
        mesh=fine,
        in_specs=(rows, rows, rows, P(), model, P(), P(), model, P(), model, held, held, rows),
        out_specs=(rows, rows, P(), model, P(), P(), model, P(), model, held, held),
        check_vma=False,
    )
```
